32 devices in a mesh: patch: 8 (over z, x), grp: 4 (over y, core).
Axes of the slice: x: 2, y: 2, z: 4, core: 2. Of those that a mesh axis runs over, the one named last changes fastest.
Arguments:
- previous: float32 [4, 8, 12, 21, 256], P('grp', 'patch'), may hold values from -4 to 4
- predicted: float32 [4, 8, 12, 21, 256], P('grp', 'patch'), may hold values from -4 to 4
- new_owner: int32 [4, 8, 12], replicated, may hold values from 0 to 7, as said below
- levels: int32 [4, 8, 12], replicated, may hold values from 0 to 2
- diffusion: float32 [21], replicated, may hold values from 0.05 to 0.5
- decay: float32 [21], replicated, may hold values from 0.1 to 1
- reaction: float32 [21, 21], replicated, may hold values from -1.25 to 1.25
Outputs:
- solution: float32 [4, 8, 16, 21, 256], P('grp', 'patch')
The draws below stay inside these ranges and needn't reach their ends.
Inputs may be any that keep to these rules, and one draw needn't show every extreme that they name: new_owner[b, o, s] is o, except that a patch of the last column of an owner o < 7 may get o + 1 and a patch of the first column of an owner o > 0 may get o - 1; at most 2 patches of one owner get o + 1 and at most 2 get o - 1; owner (0, 0) hands exactly 2 to o + 1 and owner (0, 7) exactly 2 to o - 1.
All inputs are finite; a program needn't handle non-finite values.
Results may differ from the reference program's by a relative error of at most 0.0003.
Values sent between devices are 32-bit elements; how exact they have to be, the bound alone decides.
A program may use at most 128 MiB of HBM per device.

```python
import math
import jax
import jax.numpy as jnp
from jax import lax

SPECIES = 21
CELLS = 16
ROWS_DEV = 4
COLS_DEV = 3
MOVE_CAP = 2
KRYLOV = 3
NEWTON = 2
PATCH_DEV = 12
BANDS = 4
OWNERS = 8


def draw_new_owner(key, part):
    key_right = jax.random.fold_in(key, 11)
    key_left = jax.random.fold_in(key, 12)
    key_rank_right = jax.random.fold_in(key, 13)
    key_rank_left = jax.random.fold_in(key, 14)
    owner_line = jnp.arange(OWNERS, dtype=jnp.int32)[None, :]
    right_count = jax.random.randint(key_right, (BANDS, OWNERS), 0, MOVE_CAP + 1)
    left_count = jax.random.randint(key_left, (BANDS, OWNERS), 0, MOVE_CAP + 1)
    right_count = right_count.at[0, 0].set(MOVE_CAP)
    left_count = left_count.at[0, OWNERS - 1].set(MOVE_CAP)
    right_count = jnp.where(owner_line == OWNERS - 1, 0, right_count)
    left_count = jnp.where(owner_line == 0, 0, left_count)

    def ranks_of(subkey):
        scores = jax.random.randint(subkey, (BANDS, OWNERS, ROWS_DEV), 0, 1 << 20) * ROWS_DEV + jnp.arange(ROWS_DEV, dtype=jnp.int32)
        return jnp.argsort(jnp.argsort(scores, axis=-1), axis=-1).astype(jnp.int32)
    right_move = (ranks_of(key_rank_right) < right_count[:, :, None]).astype(jnp.int32)
    left_move = (ranks_of(key_rank_left) < left_count[:, :, None]).astype(jnp.int32)
    offset = jnp.zeros((BANDS, OWNERS, ROWS_DEV, COLS_DEV), jnp.int32)
    offset = offset.at[:, :, :, COLS_DEV - 1].set(right_move)
    offset = offset.at[:, :, :, 0].add(-left_move)
    return (owner_line[:, :, None, None] + offset).reshape(BANDS, OWNERS, ROWS_DEV * COLS_DEV).astype(jnp.int32)


def with_ends(array, own_key, low, largest):
    dims = array.shape
    place = [jax.random.randint(jax.random.fold_in(own_key, axis), (), 0, dims[axis]) for axis in range(len(dims))]
    array = array.at[tuple(place)].set(low)
    longest = dims.index(max(dims))
    place[longest] = (place[longest] + 1) % dims[longest]
    return array.at[tuple(place)].set(largest)


def level_of(key, extent, pieces, low, top_value):
    factor_of, own = 1.0, jax.random.fold_in(key, 6)
    for dim, shards_of in pieces:
        draws = jnp.exp(jax.random.uniform(jax.random.fold_in(own, dim), (shards_of,), jnp.float32, low / len(pieces), top_value / len(pieces)))
        factor_of = factor_of * jnp.repeat(draws, extent[dim] // shards_of).reshape([-1 if axis == dim else 1 for axis in range(len(extent))])
    return factor_of


def normal_values(own_key, shape, scale, reach, cuts=(), kind=jnp.bfloat16):
    array = scale * jax.random.normal(own_key, shape, jnp.float32)
    if cuts:
        array = array * level_of(own_key, shape, cuts, -0.22, 0.18)
    return jnp.clip(array, -reach, reach).astype(kind)


def setup_inputs(seed: int = 0) -> dict:
    arg_keys = jax.random.split(jax.random.key(seed), 8)
    return {
        "previous": normal_values(arg_keys[0], (BANDS, OWNERS, PATCH_DEV, SPECIES, CELLS * CELLS), 1.0, 4.0, ((0, 4), (1, 8)), jnp.float32),
        "predicted": normal_values(arg_keys[1], (BANDS, OWNERS, PATCH_DEV, SPECIES, CELLS * CELLS), 1.0, 4.0, ((0, 4), (1, 8)), jnp.float32),
        "new_owner": draw_new_owner(jax.random.fold_in(arg_keys[7], 71), 0),
        "levels": with_ends(jax.random.randint(arg_keys[3], (BANDS, OWNERS, PATCH_DEV), 0, 3), jax.random.fold_in(arg_keys[3], 1), 0, 2).astype(jnp.int32),
        "diffusion": jnp.clip(jnp.exp(jax.random.uniform(arg_keys[4], (SPECIES,), jnp.float32, math.log(0.05), math.log(0.5))), 0.05, 0.5),
        "decay": jnp.clip(jnp.exp(jax.random.uniform(arg_keys[5], (SPECIES,), jnp.float32, math.log(0.1), math.log(1.0))), 0.1, 1.0),
        "reaction": normal_values(arg_keys[6], (SPECIES, SPECIES), SPECIES ** -0.5, 1.25, (), jnp.float32),
    }


step_rate = 4.0
epsilon = 1e-12
highest = lax.Precision.HIGHEST

def slot_layout(new_owner, device_rows, capacity):
    band_total, owner_total, patch_count = new_owner.shape
    device_cols = patch_count // device_rows
    owner_line = jnp.arange(owner_total, dtype=jnp.int32)[None, :, None]
    offset = new_owner - owner_line
    patch_ids = jnp.arange(band_total * owner_total * patch_count, dtype=jnp.int32).reshape(band_total, owner_total, patch_count)
    staying = jnp.where(offset == 0, patch_ids, -1)
    grid_ids = patch_ids.reshape(band_total, owner_total, device_rows, device_cols)
    grid_off = offset.reshape(band_total, owner_total, device_rows, device_cols)

    def packed(column_at, sign):
        moving = (grid_off[:, :, :, column_at] == sign).astype(jnp.int32)
        ranks = jnp.cumsum(moving, axis=-1) - 1
        choose = (moving[..., None] == 1) & (ranks[..., None] == jnp.arange(capacity, dtype=jnp.int32))
        present = jnp.any(choose, axis=2)
        summed = lax.optimization_barrier(jnp.sum(jnp.where(choose, grid_ids[:, :, :, column_at][..., None], 0), axis=2))
        return jnp.where(present, summed, -1).astype(jnp.int32)
    rightward = packed(device_cols - 1, 1)
    leftward = packed(0, -1)
    filler = jnp.full((band_total, 1, capacity), -1, jnp.int32)
    from_left = jnp.concatenate([filler, rightward[:, :-1]], axis=1)
    from_right = jnp.concatenate([leftward[:, 1:], filler], axis=1)
    return jnp.concatenate([staying, from_left, from_right], axis=2)

def conductance(level_vals):
    return jnp.where(level_vals == 0, 1.0, jnp.where(level_vals == 1, 4.0, 16.0)).astype(jnp.float32)

def to_grid(patches):
    band_total, owner_total, patch_count, species_n, surface = patches.shape
    shaped = patches.reshape(band_total, owner_total, ROWS_DEV, COLS_DEV, species_n, CELLS, CELLS)
    moved = jnp.transpose(shaped, (4, 0, 2, 5, 1, 3, 6))
    return moved.reshape(species_n, band_total * ROWS_DEV * CELLS, owner_total * COLS_DEV * CELLS)

def from_grid(grid, band_total, owner_total):
    species_n = grid.shape[0]
    shaped = grid.reshape(species_n, band_total, ROWS_DEV, CELLS, owner_total, COLS_DEV, CELLS)
    moved = jnp.transpose(shaped, (1, 4, 2, 5, 0, 3, 6))
    return moved.reshape(band_total * owner_total * ROWS_DEV * COLS_DEV, species_n, CELLS * CELLS)

def laplace(values, coeff_pad):
    padded = jnp.pad(values, ((0, 0), (1, 1), (1, 1)))
    horiz = 0.5 * (coeff_pad[1:-1, :-1] + coeff_pad[1:-1, 1:])
    vertical = 0.5 * (coeff_pad[:-1, 1:-1] + coeff_pad[1:, 1:-1])
    return horiz[:, :-1] * (padded[:, 1:-1, :-2] - values) + horiz[:, 1:] * (padded[:, 1:-1, 2:] - values) + vertical[:-1] * (padded[:, :-2, 1:-1] - values) + vertical[1:] * (padded[:, 2:, 1:-1] - values)

def small_solve(gram, rhs):
    dimension = gram.shape[0]
    matrix = gram
    vector = rhs
    for column_at in range(dimension):
        for target in range(column_at + 1, dimension):
            factor = matrix[target, column_at] / matrix[column_at, column_at]
            matrix = matrix.at[target].add(-factor * matrix[column_at])
            vector = vector.at[target].add(-factor * vector[column_at])
    answer = [None] * dimension
    for column_at in reversed(range(dimension)):
        running = vector[column_at]
        for later in range(column_at + 1, dimension):
            running = running - matrix[column_at, later] * answer[later]
        answer[column_at] = running / matrix[column_at, column_at]
    return jnp.stack(answer)

def reference(previous, predicted, new_owner, levels, diffusion, decay, reaction):
    band_total, owner_total, patch_count = new_owner.shape
    prev_grid = to_grid(previous)
    state = to_grid(predicted)
    kappa_patches = jnp.broadcast_to(conductance(levels)[:, :, :, None, None], (band_total, owner_total, patch_count, 1, CELLS * CELLS))
    coeff_pad = jnp.pad(to_grid(kappa_patches)[0], 1, mode='edge')
    differential = (jnp.arange(SPECIES) < SPECIES - 1).astype(jnp.float32)[:, None, None]
    diff_col = diffusion[:, None, None]
    decay_col = decay[:, None, None]

    def mixing(values):
        return jnp.einsum('st,tyx->syx', reaction, values, precision=highest)
    for newton_step in range(NEWTON):
        resid = differential * step_rate * (state - prev_grid) - diff_col * laplace(state, coeff_pad) - mixing(state) + decay_col * (state * state * state)
        scale = jnp.sqrt(jnp.sum(resid * resid) + epsilon)
        basis = [-resid / scale]
        curvature = 3.0 * decay_col * (state * state)
        hess = jnp.zeros((KRYLOV + 1, KRYLOV), jnp.float32)
        for column_at in range(KRYLOV):
            current = basis[column_at]
            image = differential * step_rate * current - diff_col * laplace(current, coeff_pad) - mixing(current) + curvature * current
            coeffs = [jnp.sum(image * vector) for vector in basis]
            for position in range(len(basis)):
                image = image - coeffs[position] * basis[position]
            height = jnp.sqrt(jnp.sum(image * image) + epsilon)
            hess = hess.at[:column_at + 1, column_at].set(jnp.stack(coeffs))
            hess = hess.at[column_at + 1, column_at].set(height)
            basis.append(image / height)
        gram = jnp.dot(hess.T, hess, precision=highest)
        weights = small_solve(gram, scale * hess[0])
        update = weights[0] * basis[0]
        for position in range(1, KRYLOV):
            update = update + weights[position] * basis[position]
        state = state + update
    solved = from_grid(state, band_total, owner_total)
    slot_ids = slot_layout(new_owner, ROWS_DEV, MOVE_CAP)
    picked = jnp.take(solved, jnp.maximum(slot_ids, 0).reshape(-1), axis=0)
    picked = picked.reshape(band_total, owner_total, slot_ids.shape[2], SPECIES, CELLS * CELLS)
    return jnp.where((slot_ids >= 0)[:, :, :, None, None], picked, 0.0)
```

```python
import functools

import jax
import jax.numpy as jnp
from jax import lax
from jax.experimental import pallas as pl
from jax.experimental.pallas import tpu as pltpu
from jax.sharding import PartitionSpec as P

CELLS = 16
ROWS = 4
MOVE_CAP = 2
KRYLOV = 3
NEWTON = 2

step_rate = 4.0
epsilon = 1e-12
highest = lax.Precision.HIGHEST
SHIFT = 16.0
SCALE = 64.0
PAIRS = [(i, j) for j in range(KRYLOV + 1) for i in range(j + 1)]
DIRECTIONS = [(x, y) for x in (-1, 0, 1) for y in (-1, 0, 1) if (x, y) != (0, 0)]


def small_solve(matrix, vector):
    dimension = len(vector)
    matrix = [list(line) for line in matrix]
    vector = list(vector)
    for column_at in range(dimension):
        for target in range(column_at + 1, dimension):
            factor = matrix[target][column_at] / matrix[column_at][column_at]
            for k in range(column_at, dimension):
                matrix[target][k] = matrix[target][k] - factor * matrix[column_at][k]
            vector[target] = vector[target] - factor * vector[column_at]
    answer = [None] * dimension
    for column_at in reversed(range(dimension)):
        running = vector[column_at]
        for later in range(column_at + 1, dimension):
            running = running - matrix[column_at][later] * answer[later]
        answer[column_at] = running / matrix[column_at][column_at]
    return answer


def add(a, b):
    return b if a is None else a if b is None else a + b


def total(terms):
    result = None
    for term in terms:
        result = add(result, term)
    return result


def krylov_weights(gram):
    size = KRYLOV + 1

    def inner(a, b):
        return total(
            a[i] * b[j] * gram[min(i, j), max(i, j)]
            for i in range(size)
            for j in range(size)
            if a[i] is not None and b[j] is not None
        )

    beta = jnp.sqrt(gram[0, 0] + epsilon)
    basis = [[-1.0 / beta] + [None] * KRYLOV]
    hess = [[None] * KRYLOV for _ in range(size)]
    for j in range(KRYLOV):
        current = basis[j]
        image = [None] * size
        for i in range(size):
            if current[i] is not None:
                image[i] = add(image[i], SHIFT * current[i])
                image[i + 1] = add(image[i + 1], SCALE * current[i])
        coeffs = [inner(image, vector) for vector in basis]
        for i, vector in enumerate(basis):
            hess[i][j] = coeffs[i]
            image = [
                a if b is None else a - coeffs[i] * b for a, b in zip(image, vector)
            ]
        height = jnp.sqrt(jnp.maximum(inner(image, image), 0.0) + epsilon)
        hess[j + 1][j] = height
        basis.append([None if a is None else a / height for a in image])
    normal = [
        [
            total(
                hess[k][a] * hess[k][b]
                for k in range(size)
                if hess[k][a] is not None and hess[k][b] is not None
            )
            for b in range(KRYLOV)
        ]
        for a in range(KRYLOV)
    ]
    y = small_solve(normal, [beta * hess[0][b] for b in range(KRYLOV)])
    return [
        total(y[j] * basis[j][i] for j in range(KRYLOV) if basis[j][i] is not None)
        for i in range(KRYLOV)
    ]


def kernel(
    owners, bands, owner_s, level_s, diff_in, decay_in, react_in, prev_in, pred_in, out,
    state, before, k0, k1, k2, k3, face, gram_a, gram_b, movers,
    local_sem, halo_send, halo_recv, a_send, a_recv, b_send, b_recv, move_send, move_recv,
):
    rows, cols, species, surface = prev_in.shape
    ext_rows, ext_cols = rows + 2, cols + 2
    me = lax.axis_index("patch")
    band = lax.axis_index("grp")
    MESH = pl.DeviceIdType.MESH

    def exists(dx, dy):
        tests = []
        if dx:
            tests.append(me < owners - 1 if dx > 0 else me > 0)
        if dy:
            tests.append(band < bands - 1 if dy > 0 else band > 0)
        return functools.reduce(jnp.logical_and, tests)

    barrier = pltpu.get_barrier_semaphore()
    for d in range(1, bands):
        pl.semaphore_signal(
            barrier, inc=1, device_id={"grp": lax.rem(band + d, bands)}, device_id_type=MESH
        )

    @pl.loop(1, owners)
    def _(d):
        pl.semaphore_signal(
            barrier, inc=1, device_id={"patch": lax.rem(me + d, owners)}, device_id_type=MESH
        )

    for dx, dy in DIRECTIONS:
        if dx and dy:
            @pl.when(exists(dx, dy))
            def _():
                pl.semaphore_signal(
                    barrier, inc=1, device_id={"patch": me + dx, "grp": band + dy},
                    device_id_type=MESH,
                )

    fields = ((pred_in, state), (prev_in, before))
    own = [
        pltpu.make_async_copy(
            src, dst.at[pl.ds(1, rows), pl.ds(1, cols)], local_sem.at[f]
        )
        for f, (src, dst) in enumerate(fields)
    ]
    for copy in own:
        copy.start()

    def span(delta, length):
        if delta == 0:
            return pl.ds(0, length), pl.ds(1, length)
        if delta > 0:
            return pl.ds(length - 1, 1), pl.ds(0, 1)
        return pl.ds(0, 1), pl.ds(length + 1, 1)

    def halo(f, at):
        dx, dy = DIRECTIONS[at]
        src, dst = fields[f]
        col_from, col_to = span(dx, cols)
        row_from, row_to = span(dy, rows)
        return pltpu.make_async_remote_copy(
            src_ref=src.at[row_from, col_from],
            dst_ref=dst.at[row_to, col_to],
            send_sem=halo_send.at[f, at],
            recv_sem=halo_recv.at[f, at],
            device_id={"patch": me + dx, "grp": band + dy},
            device_id_type=MESH,
        )

    def one(dx, dy):
        return jnp.where(exists(dx, dy), 1, 0)

    corners = (one(1, 0) + one(-1, 0)) * (one(0, 1) + one(0, -1))
    pl.semaphore_wait(barrier, bands - 1 + owners - 1 + corners)
    for at, (dx, dy) in enumerate(DIRECTIONS):
        @pl.when(exists(dx, dy))
        def _():
            for f in range(2):
                halo(f, at).start()

        @pl.when(jnp.logical_not(exists(-dx, -dy)))
        def _():
            row_to, col_to = span(dy, rows)[1], span(dx, cols)[1]
            shape = (row_to.size, col_to.size, species, surface)
            for f in range(2):
                fields[f][1][row_to, col_to] = jnp.zeros(shape, jnp.float32)

    lane = lax.broadcasted_iota(jnp.int32, (1, surface), 1)
    cell_col, cell_row = lane % CELLS, lane // CELLS
    west_edge, east_edge = cell_col == 0, cell_col == CELLS - 1
    south_edge, north_edge = cell_row == 0, cell_row == CELLS - 1
    diagonal = lax.broadcasted_iota(jnp.int32, (species, species), 0) == (
        lax.broadcasted_iota(jnp.int32, (species, species), 1)
    )

    def column(ref):
        return jnp.sum(jnp.where(diagonal, ref[...], 0.0), axis=1, keepdims=True)

    diffusion, decay = column(diff_in), column(decay_in)
    kind = lax.broadcasted_iota(jnp.int32, (species, 1), 0)
    rate = jnp.where(kind < species - 1, step_rate, 0.0)
    reaction = react_in[...]
    reaction_a = reaction * (1.0 / SCALE)
    diffusion_a = diffusion * (1.0 / SCALE)
    decay_a = decay * (3.0 / SCALE)
    rate_a = (rate - SHIFT) * (1.0 / SCALE)

    def kappa(r, c):
        row = jnp.clip(band * rows + r - 1, 0, bands * rows - 1)
        col = jnp.clip(me * cols + c - 1, 0, owners * cols - 1)
        level = level_s[row // rows, col // cols, (row % rows) * cols + col % cols]
        return jnp.where(level == 0, 1.0, jnp.where(level == 1, 4.0, 16.0))

    @pl.loop(0, ext_rows)
    def _(r):
        for c in range(ext_cols):
            mid = kappa(r, c)
            west = jnp.where(west_edge, 0.5 * (mid + kappa(r, c - 1)), mid)
            east = jnp.where(east_edge, 0.5 * (mid + kappa(r, c + 1)), mid)
            south = jnp.where(south_edge, 0.5 * (mid + kappa(r - 1, c)), mid)
            north = jnp.where(north_edge, 0.5 * (mid + kappa(r + 1, c)), mid)
            for d, value in enumerate((west, east, south, north)):
                face[r, c, pl.ds(d, 1), :] = value
            face[r, c, pl.ds(4, 1), :] = west + east + south + north

    for copy in own:
        copy.wait()
    for at, (dx, dy) in enumerate(DIRECTIONS):
        @pl.when(exists(-dx, -dy))
        def _():
            for f in range(2):
                halo(f, at).wait_recv()

    def inside(r, c):
        row, col = band * rows + r - 1, me * cols + c - 1
        good = (row >= 0) & (row < bands * rows) & (col >= 0) & (col < owners * cols)
        return jnp.where(good, 1.0, 0.0)

    def sweep(src, dst, finish, mix, row_from, row_to, col_from, col_to):
        @pl.loop(row_from, row_to)
        def _(r):
            below, above = jnp.maximum(r - 1, 0), jnp.minimum(r + 1, ext_rows - 1)
            for c in range(col_from, col_to):
                x = src[r, c]
                west = jnp.where(
                    west_edge,
                    pltpu.roll(src[r, max(c - 1, 0)], surface - CELLS + 1, 1),
                    pltpu.roll(x, 1, 1),
                )
                east = jnp.where(
                    east_edge,
                    pltpu.roll(src[r, min(c + 1, ext_cols - 1)], CELLS - 1, 1),
                    pltpu.roll(x, surface - 1, 1),
                )
                south = pltpu.roll(jnp.where(north_edge, src[below, c], x), CELLS, 1)
                north = pltpu.roll(jnp.where(south_edge, src[above, c], x), surface - CELLS, 1)
                lap = (
                    face[r, c, pl.ds(0, 1), :] * west
                    + face[r, c, pl.ds(1, 1), :] * east
                    + face[r, c, pl.ds(2, 1), :] * south
                    + face[r, c, pl.ds(3, 1), :] * north
                    - face[r, c, pl.ds(4, 1), :] * x
                )
                mixed = jnp.dot(mix, x, precision=highest, preferred_element_type=jnp.float32)
                dst[r, c] = finish(r, c, x, lap, mixed) * inside(r, c)

    def residual(r, c, x, lap, mixed):
        return rate * (x - before[r, c]) - diffusion * lap - mixed + decay * (x * x * x)

    def jacobian(r, c, x, lap, mixed):
        u = state[r, c]
        return (rate_a + decay_a * (u * u)) * x - diffusion_a * lap - mixed

    krylov = (k0, k1, k2, k3)
    everywhere = (0, ext_rows, 0, ext_cols)
    own_only = (1, rows + 1, 1, cols + 1)
    out_lane = lax.broadcasted_iota(jnp.int32, (1, 128), 1)

    for newton_step in range(NEWTON):
        sweep(state, k0, residual, reaction, *everywhere)
        for j in range(KRYLOV):
            sweep(
                krylov[j], krylov[j + 1], jacobian, reaction_a,
                *(everywhere if j < KRYLOV - 1 else own_only),
            )
        line = jnp.zeros((1, 128), jnp.float32)
        for at, (i, j) in enumerate(PAIRS):
            def products(r, acc, i=i, j=j):
                for c in range(1, cols + 1):
                    acc = acc + krylov[i][r, c] * krylov[j][r, c]
                return acc

            acc = lax.fori_loop(
                1, rows + 1, products, jnp.zeros((species, surface), jnp.float32)
            )
            value = jnp.sum(jnp.sum(acc, axis=0, keepdims=True), axis=1, keepdims=True)
            line = line + jnp.where(out_lane == at, value, 0.0)

        gram_a[newton_step, band] = line

        def send_a(d, slot, target):
            return pltpu.make_async_remote_copy(
                src_ref=gram_a.at[newton_step, slot],
                dst_ref=gram_a.at[newton_step, slot],
                send_sem=a_send.at[newton_step, d],
                recv_sem=a_recv.at[newton_step, d],
                device_id={"grp": target},
                device_id_type=MESH,
            )

        def send_b(d, slot, target):
            return pltpu.make_async_remote_copy(
                src_ref=gram_b.at[newton_step, slot],
                dst_ref=gram_b.at[newton_step, slot],
                send_sem=b_send.at[newton_step, d],
                recv_sem=b_recv.at[newton_step, d],
                device_id={"patch": target},
                device_id_type=MESH,
            )

        for d in range(1, bands):
            send_a(d, band, lax.rem(band + d, bands)).start()
        for d in range(1, bands):
            send_a(d, lax.rem(band + bands - d, bands), band).wait_recv()
        part = gram_a[newton_step, 0]
        for d in range(1, bands):
            part = part + gram_a[newton_step, d]
        gram_b[newton_step, me] = part

        @pl.loop(1, owners)
        def _(d):
            send_b(d, me, lax.rem(me + d, owners)).start()

        @pl.loop(1, owners)
        def _(d):
            send_b(d, lax.rem(me + owners - d, owners), me).wait_recv()

        whole = gram_b[newton_step, 0]
        for d in range(1, owners):
            whole = whole + gram_b[newton_step, d]
        gram = {
            pair: jnp.sum(jnp.where(out_lane == at, whole, 0.0), axis=1, keepdims=True)
            for at, pair in enumerate(PAIRS)
        }
        weights = [
            jnp.broadcast_to(w, (1, surface)) for w in krylov_weights(gram)
        ]

        row_from, row_to, col_from, col_to = (
            everywhere if newton_step < NEWTON - 1 else own_only
        )

        @pl.loop(row_from, row_to)
        def _(r):
            for c in range(col_from, col_to):
                state[r, c] = state[r, c] + (
                    weights[0] * k0[r, c] + weights[1] * k1[r, c] + weights[2] * k2[r, c]
                )

        for d in range(1, bands):
            send_a(d, band, band).wait_send()

        @pl.loop(1, owners)
        def _(d):
            send_b(d, me, me).wait_send()

    def new_owner(r, c):
        return owner_s[band, me, (r - 1) * cols + c - 1]

    slots = rows * cols
    for side, (c, step) in enumerate(((cols, 1), (1, -1))):
        rank = jnp.int32(0)
        packed = [jnp.zeros((species, surface), jnp.float32) for _ in range(MOVE_CAP)]
        for r in range(1, rows + 1):
            moving = new_owner(r, c) == me + step
            for m in range(MOVE_CAP):
                packed[m] = jnp.where(moving & (rank == m), state[r, c], packed[m])
            rank = rank + jnp.where(moving, 1, 0)
        for m in range(MOVE_CAP):
            movers[side, m] = packed[m]

    def move(side, step):
        return pltpu.make_async_remote_copy(
            src_ref=movers.at[side],
            dst_ref=out.at[pl.ds(slots + side * MOVE_CAP, MOVE_CAP)],
            send_sem=move_send.at[side],
            recv_sem=move_recv.at[side],
            device_id={"patch": me + step},
            device_id_type=MESH,
        )

    for side, step in enumerate((1, -1)):
        @pl.when(exists(step, 0))
        def _():
            move(side, step).start()

        @pl.when(jnp.logical_not(exists(-step, 0)))
        def _():
            out[pl.ds(slots + side * MOVE_CAP, MOVE_CAP)] = jnp.zeros(
                (MOVE_CAP, species, surface), jnp.float32
            )

    for r in range(1, rows + 1):
        for c in range(1, cols + 1):
            stays = new_owner(r, c) == me
            out[(r - 1) * cols + c - 1] = jnp.where(stays, state[r, c], 0.0)

    for at, (dx, dy) in enumerate(DIRECTIONS):
        @pl.when(exists(dx, dy))
        def _():
            for f in range(2):
                halo(f, at).wait_send()

    for side, step in enumerate((1, -1)):
        @pl.when(exists(-step, 0))
        def _():
            move(side, step).wait_recv()

        @pl.when(exists(step, 0))
        def _():
            move(side, step).wait_send()


def per_device(owners, bands, previous, predicted, new_owner, levels, diffusion, decay, reaction):
    patches, species, surface = previous.shape[2:]
    cols = patches // ROWS
    ext = (ROWS + 2, cols + 2, species, surface)
    grid = (ROWS, cols, species, surface)
    vmem = pl.BlockSpec(memory_space=pltpu.VMEM)
    smem = pl.BlockSpec(memory_space=pltpu.SMEM)
    anywhere = pl.BlockSpec(memory_space=pl.ANY)
    dma = pltpu.SemaphoreType.DMA
    result = pl.pallas_call(
        functools.partial(kernel, owners, bands),
        out_shape=jax.ShapeDtypeStruct((patches + 2 * MOVE_CAP, species, surface), jnp.float32),
        in_specs=[smem, smem, vmem, vmem, vmem, anywhere, anywhere],
        out_specs=vmem,
        scratch_shapes=[
            *[pltpu.VMEM(ext, jnp.float32) for _ in range(KRYLOV + 3)],
            pltpu.VMEM((ROWS + 2, cols + 2, 8, surface), jnp.float32),
            pltpu.VMEM((NEWTON, bands, 1, 128), jnp.float32),
            pltpu.VMEM((NEWTON, owners, 1, 128), jnp.float32),
            pltpu.VMEM((2, MOVE_CAP, species, surface), jnp.float32),
            dma((2,)),
            dma((2, len(DIRECTIONS))),
            dma((2, len(DIRECTIONS))),
            dma((NEWTON, bands)),
            dma((NEWTON, bands)),
            dma((NEWTON, owners)),
            dma((NEWTON, owners)),
            dma((2,)),
            dma((2,)),
        ],
        compiler_params=pltpu.CompilerParams(collective_id=0, has_side_effects=True),
    )(
        new_owner,
        levels,
        diffusion.reshape(1, species),
        decay.reshape(1, species),
        reaction,
        previous.reshape(grid),
        predicted.reshape(grid),
    )
    return result[None, None]


def solution(mesh):
    placed = (P("grp", "patch"), P("grp", "patch"), P(), P(), P(), P(), P())
    return jax.shard_map(
        functools.partial(per_device, mesh.shape["patch"], mesh.shape["grp"]),
        mesh=mesh,
        in_specs=placed,
        out_specs=P("grp", "patch"),
        check_vma=False,
    )
```

```python
import functools

import jax
import jax.numpy as jnp
from jax import lax
from jax.experimental import pallas as pl
from jax.experimental.pallas import tpu as pltpu
from jax.sharding import PartitionSpec as P

CELLS = 16
ROWS = 4
MOVE_CAP = 2
KRYLOV = 3
NEWTON = 2

step_rate = 4.0
epsilon = 1e-12
highest = lax.Precision.HIGHEST
SHIFT = 16.0
SCALE = 64.0
PAIRS = [(i, j) for j in range(KRYLOV + 1) for i in range(j + 1)]
DIRECTIONS = [(x, y) for x in (-1, 0, 1) for y in (-1, 0, 1) if (x, y) != (0, 0)]


def small_solve(matrix, vector):
    dimension = len(vector)
    matrix = [list(line) for line in matrix]
    vector = list(vector)
    for column_at in range(dimension):
        for target in range(column_at + 1, dimension):
            factor = matrix[target][column_at] / matrix[column_at][column_at]
            for k in range(column_at, dimension):
                matrix[target][k] = matrix[target][k] - factor * matrix[column_at][k]
            vector[target] = vector[target] - factor * vector[column_at]
    answer = [None] * dimension
    for column_at in reversed(range(dimension)):
        running = vector[column_at]
        for later in range(column_at + 1, dimension):
            running = running - matrix[column_at][later] * answer[later]
        answer[column_at] = running / matrix[column_at][column_at]
    return answer


def add(a, b):
    return b if a is None else a if b is None else a + b


def total(terms):
    result = None
    for term in terms:
        result = add(result, term)
    return result


def krylov_weights(gram):
    size = KRYLOV + 1

    def inner(a, b):
        return total(
            a[i] * b[j] * gram[min(i, j), max(i, j)]
            for i in range(size)
            for j in range(size)
            if a[i] is not None and b[j] is not None
        )

    beta = jnp.sqrt(gram[0, 0] + epsilon)
    basis = [[-1.0 / beta] + [None] * KRYLOV]
    hess = [[None] * KRYLOV for _ in range(size)]
    for j in range(KRYLOV):
        current = basis[j]
        image = [None] * size
        for i in range(size):
            if current[i] is not None:
                image[i] = add(image[i], SHIFT * current[i])
                image[i + 1] = add(image[i + 1], SCALE * current[i])
        coeffs = [inner(image, vector) for vector in basis]
        for i, vector in enumerate(basis):
            hess[i][j] = coeffs[i]
            image = [
                a if b is None else a - coeffs[i] * b for a, b in zip(image, vector)
            ]
        height = jnp.sqrt(jnp.maximum(inner(image, image), 0.0) + epsilon)
        hess[j + 1][j] = height
        basis.append([None if a is None else a / height for a in image])
    normal = [
        [
            total(
                hess[k][a] * hess[k][b]
                for k in range(size)
                if hess[k][a] is not None and hess[k][b] is not None
            )
            for b in range(KRYLOV)
        ]
        for a in range(KRYLOV)
    ]
    y = small_solve(normal, [beta * hess[0][b] for b in range(KRYLOV)])
    return [
        total(y[j] * basis[j][i] for j in range(KRYLOV) if basis[j][i] is not None)
        for i in range(KRYLOV)
    ]


def kernel(
    owners, bands, owner_s, level_s, diff_in, decay_in, react_in, prev_in, pred_in, out,
    state, before, k0, k1, k2, k3, face, gram_a, gram_b, movers, landing, strip_out, strip_in,
    local_sem, halo_send, halo_recv, a_send, a_recv, b_send, b_recv, move_send, move_recv,
):
    rows, cols, species, surface = prev_in.shape
    ext_rows, ext_cols = rows + 2, cols + 2
    me = lax.axis_index("patch")
    band = lax.axis_index("grp")
    MESH = pl.DeviceIdType.MESH

    def exists(dx, dy):
        tests = []
        if dx:
            tests.append(me < owners - 1 if dx > 0 else me > 0)
        if dy:
            tests.append(band < bands - 1 if dy > 0 else band > 0)
        return functools.reduce(jnp.logical_and, tests)

    barrier = pltpu.get_barrier_semaphore()
    for d in range(1, bands):
        pl.semaphore_signal(
            barrier, inc=1, device_id={"grp": lax.rem(band + d, bands)}, device_id_type=MESH
        )

    @pl.loop(1, owners)
    def _(d):
        pl.semaphore_signal(
            barrier, inc=1, device_id={"patch": lax.rem(me + d, owners)}, device_id_type=MESH
        )

    for dx, dy in DIRECTIONS:
        if dx and dy:
            @pl.when(exists(dx, dy))
            def _():
                pl.semaphore_signal(
                    barrier, inc=1, device_id={"patch": me + dx, "grp": band + dy},
                    device_id_type=MESH,
                )

    fields = ((pred_in, state), (prev_in, before))
    own = [
        pltpu.make_async_copy(
            src, dst.at[pl.ds(1, rows), pl.ds(1, cols)], local_sem.at[f]
        )
        for f, (src, dst) in enumerate(fields)
    ]
    for copy in own:
        copy.start()

    half = surface // 2
    low, high = pl.ds(0, half), pl.ds(half, half)
    pairs = rows // 2

    def span(delta, length):
        if delta == 0:
            return pl.ds(0, length), pl.ds(1, length)
        if delta > 0:
            return pl.ds(length - 1, 1), pl.ds(0, 1)
        return pl.ds(0, 1), pl.ds(length + 1, 1)

    def halo(f, at):
        dx, dy = DIRECTIONS[at]
        src, dst = fields[f]
        if dy == 0:
            side = 0 if dx > 0 else 1
            source, target = strip_out.at[f, side], strip_in.at[f, side]
        else:
            lanes = high if dy > 0 else low
            col_from, col_to = span(dx, cols)
            row_from, row_to = span(dy, rows)
            source = src.at[row_from, col_from, :, lanes]
            target = dst.at[row_to, col_to, :, lanes]
        return pltpu.make_async_remote_copy(
            src_ref=source,
            dst_ref=target,
            send_sem=halo_send.at[f, at],
            recv_sem=halo_recv.at[f, at],
            device_id={"patch": me + dx, "grp": band + dy},
            device_id_type=MESH,
        )

    lane = lax.broadcasted_iota(jnp.int32, (1, surface), 1)
    cell_col, cell_row = lane % CELLS, lane // CELLS
    right_half = cell_col >= CELLS // 2

    for copy in own:
        copy.wait()
    for f in range(2):
        field = fields[f][1]
        for k in range(pairs):
            first, second = field[2 * k + 1, cols], field[2 * k + 2, cols]
            strip_out[f, 0, k] = jnp.where(
                right_half, first, pltpu.roll(second, surface - CELLS // 2, 1)
            )
            first, second = field[2 * k + 1, 1], field[2 * k + 2, 1]
            strip_out[f, 1, k] = jnp.where(
                right_half, pltpu.roll(second, CELLS // 2, 1), first
            )

    def one(dx, dy):
        return jnp.where(exists(dx, dy), 1, 0)

    corners = (one(1, 0) + one(-1, 0)) * (one(0, 1) + one(0, -1))
    pl.semaphore_wait(barrier, bands - 1 + owners - 1 + corners)
    for at, (dx, dy) in enumerate(DIRECTIONS):
        @pl.when(exists(dx, dy))
        def _():
            for f in range(2):
                halo(f, at).start()

        @pl.when(jnp.logical_not(exists(-dx, -dy)))
        def _():
            row_to, col_to = span(dy, rows)[1], span(dx, cols)[1]
            lanes = pl.ds(0, surface) if dy == 0 else high if dy > 0 else low
            shape = (row_to.size, col_to.size, species, lanes.size)
            for f in range(2):
                fields[f][1][row_to, col_to, :, lanes] = jnp.zeros(shape, jnp.float32)

    west_edge, east_edge = cell_col == 0, cell_col == CELLS - 1
    south_edge, north_edge = cell_row == 0, cell_row == CELLS - 1
    diagonal = lax.broadcasted_iota(jnp.int32, (species, species), 0) == (
        lax.broadcasted_iota(jnp.int32, (species, species), 1)
    )

    def column(ref):
        return jnp.sum(jnp.where(diagonal, ref[...], 0.0), axis=1, keepdims=True)

    diffusion, decay = column(diff_in), column(decay_in)
    kind = lax.broadcasted_iota(jnp.int32, (species, 1), 0)
    rate = jnp.where(kind < species - 1, step_rate, 0.0)
    reaction = react_in[...]
    reaction_a = reaction * (1.0 / SCALE)
    diffusion_a = diffusion * (1.0 / SCALE)
    decay_a = decay * (3.0 / SCALE)
    rate_a = (rate - SHIFT) * (1.0 / SCALE)

    def kappa(r, c):
        row = jnp.clip(band * rows + r - 1, 0, bands * rows - 1)
        col = jnp.clip(me * cols + c - 1, 0, owners * cols - 1)
        level = level_s[row // rows, col // cols, (row % rows) * cols + col % cols]
        return jnp.where(level == 0, 1.0, jnp.where(level == 1, 4.0, 16.0))

    @pl.loop(0, ext_rows)
    def _(r):
        for c in range(ext_cols):
            mid = kappa(r, c)
            west = jnp.where(west_edge, 0.5 * (mid + kappa(r, c - 1)), mid)
            east = jnp.where(east_edge, 0.5 * (mid + kappa(r, c + 1)), mid)
            south = jnp.where(south_edge, 0.5 * (mid + kappa(r - 1, c)), mid)
            north = jnp.where(north_edge, 0.5 * (mid + kappa(r + 1, c)), mid)
            for d, value in enumerate((west, east, south, north)):
                face[r, c, pl.ds(d, 1), :] = value
            face[r, c, pl.ds(4, 1), :] = west + east + south + north

    for at, (dx, dy) in enumerate(DIRECTIONS):
        @pl.when(exists(-dx, -dy))
        def _():
            for f in range(2):
                halo(f, at).wait_recv()
            if dy == 0:
                for f in range(2):
                    for k in range(pairs):
                        strip = strip_in[f, 0 if dx > 0 else 1, k]
                        at_col = 0 if dx > 0 else cols + 1
                        shift = CELLS // 2 if dx > 0 else surface - CELLS // 2
                        fields[f][1][2 * k + 1, at_col] = strip
                        fields[f][1][2 * k + 2, at_col] = pltpu.roll(strip, shift, 1)

    def inside(r, c):
        row, col = band * rows + r - 1, me * cols + c - 1
        good = (row >= 0) & (row < bands * rows) & (col >= 0) & (col < owners * cols)
        return jnp.where(good, 1.0, 0.0)

    def edges(width):
        column = lax.broadcasted_iota(jnp.int32, (1, width), 1)
        return (
            column % CELLS == 0,
            column % CELLS == CELLS - 1,
            column < CELLS,
            column >= width - CELLS,
        )

    whole_edges, half_edges = edges(surface), edges(half)

    def patch(src, dst, finish, r, c, lanes, below, above):
        width = lanes.size
        at_west, at_east, at_south, at_north = (
            whole_edges if width == surface else half_edges
        )
        x = src[r, c, :, lanes]
        left = src[r, max(c - 1, 0), :, lanes]
        right = src[r, min(c + 1, ext_cols - 1), :, lanes]
        under = x if below is None else src[below[0], c, :, below[1]]
        over = x if above is None else src[above[0], c, :, above[1]]
        west = jnp.where(
            at_west, pltpu.roll(left, width - CELLS + 1, 1), pltpu.roll(x, 1, 1)
        )
        east = jnp.where(
            at_east, pltpu.roll(right, CELLS - 1, 1), pltpu.roll(x, width - 1, 1)
        )
        south = pltpu.roll(jnp.where(at_north, under, x), CELLS, 1)
        north = pltpu.roll(jnp.where(at_south, over, x), width - CELLS, 1)
        lap = (
            face[r, c, pl.ds(0, 1), lanes] * west
            + face[r, c, pl.ds(1, 1), lanes] * east
            + face[r, c, pl.ds(2, 1), lanes] * south
            + face[r, c, pl.ds(3, 1), lanes] * north
            - face[r, c, pl.ds(4, 1), lanes] * x
        )
        dst[r, c, :, lanes] = finish(r, c, lanes, x, lap)

    full = pl.ds(0, surface)

    def sweep(src, dst, finish, ring):
        col_from, col_to = (0, ext_cols) if ring else (1, cols + 1)

        def masked(r, c, lanes, x, lap):
            return finish(r, c, lanes, x, lap) * inside(r, c)

        last = ext_rows - 1
        if ring:
            for c in range(ext_cols):
                patch(src, dst, masked, 0, c, high, None, (1, low))
                patch(src, dst, masked, last, c, low, (last - 1, high), None)

        @pl.loop(1, rows + 1)
        def _(r):
            for c in range(col_from, col_to):
                patch(
                    src, dst, masked if c in (0, cols + 1) else finish,
                    r, c, full, (r - 1, full), (r + 1, full),
                )

    def split(value):
        big = value.astype(jnp.bfloat16)
        return big, (value - big.astype(jnp.float32)).astype(jnp.bfloat16)

    react_big, react_small = split(reaction_a)

    def mixing(x):
        big, small = split(x)

        def product(a, b):
            return jnp.dot(a, b, preferred_element_type=jnp.float32)

        return product(react_small, big) + product(react_big, small) + product(react_big, big)

    def residual(r, c, lanes, x, lap):
        mixed = jnp.dot(reaction, x, precision=highest, preferred_element_type=jnp.float32)
        old = before[r, c, :, lanes]
        return rate * (x - old) - diffusion * lap - mixed + decay * (x * x * x)

    def jacobian(r, c, lanes, x, lap):
        u = state[r, c, :, lanes]
        return (rate_a + decay_a * (u * u)) * x - diffusion_a * lap - mixing(x)

    krylov = (k0, k1, k2, k3)
    out_lane = lax.broadcasted_iota(jnp.int32, (1, 128), 1)

    def new_owner(r, c):
        return owner_s[band, me, (r - 1) * cols + c - 1]

    slots = rows * cols

    def move(part, side, step):
        return pltpu.make_async_remote_copy(
            src_ref=movers.at[part, side],
            dst_ref=landing.at[part, side],
            send_sem=move_send.at[part, side],
            recv_sem=move_recv.at[part, side],
            device_id={"patch": me + step},
            device_id_type=MESH,
        )

    def send_movers(part, field):
        for side, (c, step) in enumerate(((cols, 1), (1, -1))):
            rank = jnp.int32(0)
            packed = [jnp.zeros((species, surface), jnp.float32) for _ in range(MOVE_CAP)]
            for r in range(1, rows + 1):
                moving = new_owner(r, c) == me + step
                for m in range(MOVE_CAP):
                    packed[m] = jnp.where(moving & (rank == m), field[r, c], packed[m])
                rank = rank + jnp.where(moving, 1, 0)
            for m in range(MOVE_CAP):
                movers[part, side, m] = packed[m]
        for side, step in enumerate((1, -1)):
            @pl.when(exists(step, 0))
            def _():
                move(part, side, step).start()

    for newton_step in range(NEWTON):
        final = newton_step == NEWTON - 1
        if final:
            send_movers(0, state)
        sweep(state, k0, residual, True)
        for j in range(KRYLOV):
            if final:
                send_movers(j + 1, krylov[j])
            sweep(krylov[j], krylov[j + 1], jacobian, j < KRYLOV - 1)
        line = jnp.zeros((1, 128), jnp.float32)
        for at, (i, j) in enumerate(PAIRS):
            def products(r, acc, i=i, j=j):
                for c in range(1, cols + 1):
                    acc = acc + krylov[i][r, c] * krylov[j][r, c]
                return acc

            acc = lax.fori_loop(
                1, rows + 1, products, jnp.zeros((species, surface), jnp.float32)
            )
            value = jnp.sum(jnp.sum(acc, axis=0, keepdims=True), axis=1, keepdims=True)
            line = line + jnp.where(out_lane == at, value, 0.0)

        gram_a[newton_step, band] = line

        def send_a(d, slot, target):
            return pltpu.make_async_remote_copy(
                src_ref=gram_a.at[newton_step, slot],
                dst_ref=gram_a.at[newton_step, slot],
                send_sem=a_send.at[newton_step, d],
                recv_sem=a_recv.at[newton_step, d],
                device_id={"grp": target},
                device_id_type=MESH,
            )

        def send_b(d, slot, target):
            return pltpu.make_async_remote_copy(
                src_ref=gram_b.at[newton_step, slot],
                dst_ref=gram_b.at[newton_step, slot],
                send_sem=b_send.at[newton_step, d],
                recv_sem=b_recv.at[newton_step, d],
                device_id={"patch": target},
                device_id_type=MESH,
            )

        for d in range(1, bands):
            send_a(d, band, lax.rem(band + d, bands)).start()
        for d in range(1, bands):
            send_a(d, lax.rem(band + bands - d, bands), band).wait_recv()
        part = gram_a[newton_step, 0]
        for d in range(1, bands):
            part = part + gram_a[newton_step, d]
        gram_b[newton_step, me] = part

        @pl.loop(1, owners)
        def _(d):
            send_b(d, me, lax.rem(me + d, owners)).start()

        @pl.loop(1, owners)
        def _(d):
            send_b(d, lax.rem(me + owners - d, owners), me).wait_recv()

        whole = gram_b[newton_step, 0]
        for d in range(1, owners):
            whole = whole + gram_b[newton_step, d]
        gram = {
            pair: jnp.sum(jnp.where(out_lane == at, whole, 0.0), axis=1, keepdims=True)
            for at, pair in enumerate(PAIRS)
        }
        weights = [
            jnp.broadcast_to(w, (1, surface)) for w in krylov_weights(gram)
        ]

        def update(r, c, lanes):
            return state[r, c, :, lanes] + (
                weights[0][:, : lanes.size] * k0[r, c, :, lanes]
                + weights[1][:, : lanes.size] * k1[r, c, :, lanes]
                + weights[2][:, : lanes.size] * k2[r, c, :, lanes]
            )

        if not final:
            for c in range(ext_cols):
                state[0, c, :, high] = update(0, c, high)
                state[ext_rows - 1, c, :, low] = update(ext_rows - 1, c, low)

            @pl.loop(1, rows + 1)
            def _(r):
                for c in range(ext_cols):
                    state[r, c] = update(r, c, full)
        else:
            @pl.loop(1, rows + 1)
            def _(r):
                for c in range(1, cols + 1):
                    stays = new_owner(r, c) == me
                    out[(r - 1) * cols + c - 1] = jnp.where(stays, update(r, c, full), 0.0)

        for d in range(1, bands):
            send_a(d, band, band).wait_send()

        @pl.loop(1, owners)
        def _(d):
            send_b(d, me, me).wait_send()

    for side, step in enumerate((1, -1)):
        place = slots + side * MOVE_CAP

        @pl.when(exists(-step, 0))
        def _():
            for part in range(KRYLOV + 1):
                move(part, side, step).wait_recv()
            for m in range(MOVE_CAP):
                out[place + m] = landing[0, side, m] + (
                    weights[0] * landing[1, side, m]
                    + weights[1] * landing[2, side, m]
                    + weights[2] * landing[3, side, m]
                )

        @pl.when(jnp.logical_not(exists(-step, 0)))
        def _():
            out[pl.ds(place, MOVE_CAP)] = jnp.zeros((MOVE_CAP, species, surface), jnp.float32)

        @pl.when(exists(step, 0))
        def _():
            for part in range(KRYLOV + 1):
                move(part, side, step).wait_send()

    for at, (dx, dy) in enumerate(DIRECTIONS):
        @pl.when(exists(dx, dy))
        def _():
            for f in range(2):
                halo(f, at).wait_send()


def per_device(owners, bands, previous, predicted, new_owner, levels, diffusion, decay, reaction):
    patches, species, surface = previous.shape[2:]
    cols = patches // ROWS
    ext = (ROWS + 2, cols + 2, species, surface)
    grid = (ROWS, cols, species, surface)
    vmem = pl.BlockSpec(memory_space=pltpu.VMEM)
    smem = pl.BlockSpec(memory_space=pltpu.SMEM)
    anywhere = pl.BlockSpec(memory_space=pl.ANY)
    dma = pltpu.SemaphoreType.DMA
    result = pl.pallas_call(
        functools.partial(kernel, owners, bands),
        out_shape=jax.ShapeDtypeStruct((patches + 2 * MOVE_CAP, species, surface), jnp.float32),
        in_specs=[smem, smem, vmem, vmem, vmem, anywhere, anywhere],
        out_specs=vmem,
        scratch_shapes=[
            *[pltpu.VMEM(ext, jnp.float32) for _ in range(KRYLOV + 3)],
            pltpu.VMEM((ROWS + 2, cols + 2, 8, surface), jnp.float32),
            pltpu.VMEM((NEWTON, bands, 1, 128), jnp.float32),
            pltpu.VMEM((NEWTON, owners, 1, 128), jnp.float32),
            pltpu.VMEM((KRYLOV + 1, 2, MOVE_CAP, species, surface), jnp.float32),
            pltpu.VMEM((KRYLOV + 1, 2, MOVE_CAP, species, surface), jnp.float32),
            pltpu.VMEM((2, 2, ROWS // 2, species, surface), jnp.float32),
            pltpu.VMEM((2, 2, ROWS // 2, species, surface), jnp.float32),
            dma((2,)),
            dma((2, len(DIRECTIONS))),
            dma((2, len(DIRECTIONS))),
            dma((NEWTON, bands)),
            dma((NEWTON, bands)),
            dma((NEWTON, owners)),
            dma((NEWTON, owners)),
            dma((KRYLOV + 1, 2)),
            dma((KRYLOV + 1, 2)),
        ],
        compiler_params=pltpu.CompilerParams(collective_id=0, has_side_effects=True),
    )(
        new_owner,
        levels,
        diffusion.reshape(1, species),
        decay.reshape(1, species),
        reaction,
        previous.reshape(grid),
        predicted.reshape(grid),
    )
    return result[None, None]


def solution(mesh):
    placed = (P("grp", "patch"), P("grp", "patch"), P(), P(), P(), P(), P())
    return jax.shard_map(
        functools.partial(per_device, mesh.shape["patch"], mesh.shape["grp"]),
        mesh=mesh,
        in_specs=placed,
        out_specs=P("grp", "patch"),
        check_vma=False,
    )
```

```python
import functools

import jax
import jax.numpy as jnp
from jax import lax
from jax.experimental import pallas as pl
from jax.experimental.pallas import tpu as pltpu
from jax.sharding import PartitionSpec as P

CELLS = 16
ROWS = 4
MOVE_CAP = 2
KRYLOV = 3
NEWTON = 2

step_rate = 4.0
epsilon = 1e-12
highest = lax.Precision.HIGHEST
SHIFT = 16.0
SCALE = 64.0
PAIRS = [(i, j) for j in range(KRYLOV + 1) for i in range(j + 1)]
DIRECTIONS = [(x, y) for x in (-1, 0, 1) for y in (-1, 0, 1) if (x, y) != (0, 0)]


def small_solve(matrix, vector):
    dimension = len(vector)
    matrix = [list(line) for line in matrix]
    vector = list(vector)
    for column_at in range(dimension):
        for target in range(column_at + 1, dimension):
            factor = matrix[target][column_at] / matrix[column_at][column_at]
            for k in range(column_at, dimension):
                matrix[target][k] = matrix[target][k] - factor * matrix[column_at][k]
            vector[target] = vector[target] - factor * vector[column_at]
    answer = [None] * dimension
    for column_at in reversed(range(dimension)):
        running = vector[column_at]
        for later in range(column_at + 1, dimension):
            running = running - matrix[column_at][later] * answer[later]
        answer[column_at] = running / matrix[column_at][column_at]
    return answer


def add(a, b):
    return b if a is None else a if b is None else a + b


def total(terms):
    result = None
    for term in terms:
        result = add(result, term)
    return result


def krylov_weights(gram):
    size = KRYLOV + 1

    def inner(a, b):
        return total(
            a[i] * b[j] * gram[min(i, j), max(i, j)]
            for i in range(size)
            for j in range(size)
            if a[i] is not None and b[j] is not None
        )

    beta = jnp.sqrt(gram[0, 0] + epsilon)
    basis = [[-1.0 / beta] + [None] * KRYLOV]
    hess = [[None] * KRYLOV for _ in range(size)]
    for j in range(KRYLOV):
        current = basis[j]
        image = [None] * size
        for i in range(size):
            if current[i] is not None:
                image[i] = add(image[i], SHIFT * current[i])
                image[i + 1] = add(image[i + 1], SCALE * current[i])
        coeffs = [inner(image, vector) for vector in basis]
        for i, vector in enumerate(basis):
            hess[i][j] = coeffs[i]
            image = [
                a if b is None else a - coeffs[i] * b for a, b in zip(image, vector)
            ]
        height = jnp.sqrt(jnp.maximum(inner(image, image), 0.0) + epsilon)
        hess[j + 1][j] = height
        basis.append([None if a is None else a / height for a in image])
    normal = [
        [
            total(
                hess[k][a] * hess[k][b]
                for k in range(size)
                if hess[k][a] is not None and hess[k][b] is not None
            )
            for b in range(KRYLOV)
        ]
        for a in range(KRYLOV)
    ]
    y = small_solve(normal, [beta * hess[0][b] for b in range(KRYLOV)])
    return [
        total(y[j] * basis[j][i] for j in range(KRYLOV) if basis[j][i] is not None)
        for i in range(KRYLOV)
    ]


def kernel(
    owners, bands, owner_s, level_s, diff_in, decay_in, react_in, prev_in, pred_in, out,
    state, before, k0, k1, k2, k3, face, gram_a, gram_b, movers, landing, strip_out, strip_in, stage,
    local_sem, halo_send, halo_recv, a_send, a_recv, b_send, b_recv, move_send, move_recv,
):
    ext_rows, ext_cols, species, surface = state.shape
    rows, cols = ext_rows - 2, ext_cols - 2
    me = lax.axis_index("patch")
    band = lax.axis_index("grp")
    MESH = pl.DeviceIdType.MESH

    def exists(dx, dy):
        tests = []
        if dx:
            tests.append(me < owners - 1 if dx > 0 else me > 0)
        if dy:
            tests.append(band < bands - 1 if dy > 0 else band > 0)
        return functools.reduce(jnp.logical_and, tests)

    barrier = pltpu.get_barrier_semaphore()
    for d in range(1, bands):
        pl.semaphore_signal(
            barrier, inc=1, device_id={"grp": lax.rem(band + d, bands)}, device_id_type=MESH
        )

    @pl.loop(1, owners)
    def _(d):
        pl.semaphore_signal(
            barrier, inc=1, device_id={"patch": lax.rem(me + d, owners)}, device_id_type=MESH
        )

    for dx, dy in DIRECTIONS:
        if dx and dy:
            @pl.when(exists(dx, dy))
            def _():
                pl.semaphore_signal(
                    barrier, inc=1, device_id={"patch": me + dx, "grp": band + dy},
                    device_id_type=MESH,
                )

    fields = ((pred_in, state), (prev_in, before))
    own = [
        pltpu.make_async_copy(src, stage.at[f], local_sem.at[f])
        for f, (src, dst) in enumerate(fields)
    ]
    for copy in own:
        copy.start()

    half = surface // 2
    low, high = pl.ds(0, half), pl.ds(half, half)
    pairs = rows // 2

    def span(delta, length):
        if delta == 0:
            return pl.ds(1, length), pl.ds(1, length)
        if delta > 0:
            return pl.ds(length, 1), pl.ds(0, 1)
        return pl.ds(1, 1), pl.ds(length + 1, 1)

    def halo(f, at):
        dx, dy = DIRECTIONS[at]
        field = fields[f][1]
        if dy == 0:
            side = 0 if dx > 0 else 1
            source, target = strip_out.at[f, side], strip_in.at[f, side]
        else:
            lanes = high if dy > 0 else low
            col_from, col_to = span(dx, cols)
            row_from, row_to = span(dy, rows)
            source = field.at[row_from, col_from, :, lanes]
            target = field.at[row_to, col_to, :, lanes]
        return pltpu.make_async_remote_copy(
            src_ref=source,
            dst_ref=target,
            send_sem=halo_send.at[f, at],
            recv_sem=halo_recv.at[f, at],
            device_id={"patch": me + dx, "grp": band + dy},
            device_id_type=MESH,
        )

    lane = lax.broadcasted_iota(jnp.int32, (1, surface), 1)
    cell_col, cell_row = lane % CELLS, lane // CELLS
    right_half = cell_col >= CELLS // 2

    for f in range(2):
        own[f].wait()
        field = fields[f][1]
        for r in range(rows):
            for c in range(cols):
                for part, lanes in enumerate((low, high)):
                    first = (r * cols + c) * species * 2 + part
                    field[r + 1, c + 1, :, lanes] = stage[
                        f, pl.ds(first, species, stride=2), :
                    ]
        for k in range(pairs):
            first, second = field[2 * k + 1, cols], field[2 * k + 2, cols]
            strip_out[f, 0, k] = jnp.where(
                right_half, first, pltpu.roll(second, surface - CELLS // 2, 1)
            )
            first, second = field[2 * k + 1, 1], field[2 * k + 2, 1]
            strip_out[f, 1, k] = jnp.where(
                right_half, pltpu.roll(second, CELLS // 2, 1), first
            )

    def one(dx, dy):
        return jnp.where(exists(dx, dy), 1, 0)

    corners = (one(1, 0) + one(-1, 0)) * (one(0, 1) + one(0, -1))
    pl.semaphore_wait(barrier, bands - 1 + owners - 1 + corners)
    for at, (dx, dy) in enumerate(DIRECTIONS):
        @pl.when(exists(dx, dy))
        def _():
            halo(0, at).start()

        @pl.when(jnp.logical_not(exists(-dx, -dy)))
        def _():
            row_to, col_to = span(dy, rows)[1], span(dx, cols)[1]
            lanes = pl.ds(0, surface) if dy == 0 else high if dy > 0 else low
            shape = (row_to.size, col_to.size, species, lanes.size)
            for f in range(2):
                fields[f][1][row_to, col_to, :, lanes] = jnp.zeros(shape, jnp.float32)

    for at, (dx, dy) in enumerate(DIRECTIONS):
        @pl.when(exists(dx, dy))
        def _():
            halo(1, at).start()

    west_edge, east_edge = cell_col == 0, cell_col == CELLS - 1
    south_edge, north_edge = cell_row == 0, cell_row == CELLS - 1
    diagonal = lax.broadcasted_iota(jnp.int32, (species, species), 0) == (
        lax.broadcasted_iota(jnp.int32, (species, species), 1)
    )

    def column(ref):
        return jnp.sum(jnp.where(diagonal, ref[...], 0.0), axis=1, keepdims=True)

    diffusion, decay = column(diff_in), column(decay_in)
    kind = lax.broadcasted_iota(jnp.int32, (species, 1), 0)
    rate = jnp.where(kind < species - 1, step_rate, 0.0)
    reaction = react_in[...]
    reaction_a = reaction * (1.0 / SCALE)
    diffusion_a = diffusion * (1.0 / SCALE)
    decay_a = decay * (3.0 / SCALE)
    rate_a = (rate - SHIFT) * (1.0 / SCALE)

    def kappa(r, c):
        row = jnp.clip(band * rows + r - 1, 0, bands * rows - 1)
        col = jnp.clip(me * cols + c - 1, 0, owners * cols - 1)
        level = level_s[row // rows, col // cols, (row % rows) * cols + col % cols]
        return jnp.where(level == 0, 1.0, jnp.where(level == 1, 4.0, 16.0))

    @pl.loop(0, ext_rows)
    def _(r):
        for c in range(ext_cols):
            mid = kappa(r, c)
            west = jnp.where(west_edge, 0.5 * (mid + kappa(r, c - 1)), mid)
            east = jnp.where(east_edge, 0.5 * (mid + kappa(r, c + 1)), mid)
            south = jnp.where(south_edge, 0.5 * (mid + kappa(r - 1, c)), mid)
            north = jnp.where(north_edge, 0.5 * (mid + kappa(r + 1, c)), mid)
            for d, value in enumerate((west, east, south, north)):
                face[r, c, pl.ds(d, 1), :] = value
            face[r, c, pl.ds(4, 1), :] = west + east + south + north

    def receive(f):
        for at, (dx, dy) in enumerate(DIRECTIONS):
            @pl.when(exists(-dx, -dy))
            def _():
                halo(f, at).wait_recv()
                if dy == 0:
                    for k in range(pairs):
                        strip = strip_in[f, 0 if dx > 0 else 1, k]
                        at_col = 0 if dx > 0 else cols + 1
                        shift = CELLS // 2 if dx > 0 else surface - CELLS // 2
                        fields[f][1][2 * k + 1, at_col] = strip
                        fields[f][1][2 * k + 2, at_col] = pltpu.roll(strip, shift, 1)

    def inside(r, c):
        row, col = band * rows + r - 1, me * cols + c - 1
        good = (row >= 0) & (row < bands * rows) & (col >= 0) & (col < owners * cols)
        return jnp.where(good, 1.0, 0.0)

    def edges(width):
        column = lax.broadcasted_iota(jnp.int32, (1, width), 1)
        return (
            column % CELLS == 0,
            column % CELLS == CELLS - 1,
            column < CELLS,
            column >= width - CELLS,
        )

    whole_edges, half_edges = edges(surface), edges(half)

    def patch(src, dst, finish, r, c, lanes, below, above):
        width = lanes.size
        at_west, at_east, at_south, at_north = (
            whole_edges if width == surface else half_edges
        )
        x = src[r, c, :, lanes]
        left = src[r, max(c - 1, 0), :, lanes]
        right = src[r, min(c + 1, ext_cols - 1), :, lanes]
        under = x if below is None else src[below[0], c, :, below[1]]
        over = x if above is None else src[above[0], c, :, above[1]]
        west = jnp.where(
            at_west, pltpu.roll(left, width - CELLS + 1, 1), pltpu.roll(x, 1, 1)
        )
        east = jnp.where(
            at_east, pltpu.roll(right, CELLS - 1, 1), pltpu.roll(x, width - 1, 1)
        )
        south = pltpu.roll(jnp.where(at_north, under, x), CELLS, 1)
        north = pltpu.roll(jnp.where(at_south, over, x), width - CELLS, 1)
        lap = (
            face[r, c, pl.ds(0, 1), lanes] * west
            + face[r, c, pl.ds(1, 1), lanes] * east
            + face[r, c, pl.ds(2, 1), lanes] * south
            + face[r, c, pl.ds(3, 1), lanes] * north
            - face[r, c, pl.ds(4, 1), lanes] * x
        )
        dst[r, c, :, lanes] = finish(r, c, lanes, x, lap)

    full = pl.ds(0, surface)

    def sweep(src, dst, finish, own=True, ring=True):
        columns = list(range(1, cols + 1)) if own else []
        if ring:
            columns = [0, *columns, cols + 1]

        def masked(r, c, lanes, x, lap):
            return finish(r, c, lanes, x, lap) * inside(r, c)

        last = ext_rows - 1
        if ring:
            for c in range(ext_cols):
                patch(src, dst, masked, 0, c, high, None, (1, low))
                patch(src, dst, masked, last, c, low, (last - 1, high), None)

        @pl.loop(1, rows + 1)
        def _(r):
            for c in columns:
                patch(
                    src, dst, masked if c in (0, cols + 1) else finish,
                    r, c, full, (r - 1, full), (r + 1, full),
                )

    def split(value):
        big = value.astype(jnp.bfloat16)
        return big, (value - big.astype(jnp.float32)).astype(jnp.bfloat16)

    react_big, react_small = split(reaction_a)

    def mixing(x):
        big, small = split(x)

        def product(a, b):
            return jnp.dot(a, b, preferred_element_type=jnp.float32)

        return product(react_small, big) + product(react_big, small) + product(react_big, big)

    def residual(r, c, lanes, x, lap):
        mixed = jnp.dot(reaction, x, precision=highest, preferred_element_type=jnp.float32)
        old = before[r, c, :, lanes]
        return rate * (x - old) - diffusion * lap - mixed + decay * (x * x * x)

    def jacobian(r, c, lanes, x, lap):
        u = state[r, c, :, lanes]
        return (rate_a + decay_a * (u * u)) * x - diffusion_a * lap - mixing(x)

    krylov = (k0, k1, k2, k3)
    out_lane = lax.broadcasted_iota(jnp.int32, (1, 128), 1)

    def new_owner(r, c):
        return owner_s[band, me, (r - 1) * cols + c - 1]

    slots = rows * cols

    def emit(slot, value):
        for part in range(2):
            first = slot // 8 * 16 + part * 8 + slot % 8
            out[pl.ds(first, species, stride=2 * (slots + 2 * MOVE_CAP)), :] = (
                value[:, part * half : (part + 1) * half]
            )

    def move(part, side, step):
        return pltpu.make_async_remote_copy(
            src_ref=movers.at[part, side],
            dst_ref=landing.at[part, side],
            send_sem=move_send.at[part, side],
            recv_sem=move_recv.at[part, side],
            device_id={"patch": me + step},
            device_id_type=MESH,
        )

    def send_movers(part, field):
        for side, (c, step) in enumerate(((cols, 1), (1, -1))):
            rank = jnp.int32(0)
            packed = [jnp.zeros((species, surface), jnp.float32) for _ in range(MOVE_CAP)]
            for r in range(1, rows + 1):
                moving = new_owner(r, c) == me + step
                for m in range(MOVE_CAP):
                    packed[m] = jnp.where(moving & (rank == m), field[r, c], packed[m])
                rank = rank + jnp.where(moving, 1, 0)
            for m in range(MOVE_CAP):
                movers[part, side, m] = packed[m]
        for side, step in enumerate((1, -1)):
            @pl.when(exists(step, 0))
            def _():
                move(part, side, step).start()

    for newton_step in range(NEWTON):
        final = newton_step == NEWTON - 1
        if final:
            send_movers(0, state)
        if newton_step == 0:
            receive(0)
            sweep(state, k0, residual, ring=False)
            receive(1)
            sweep(state, k0, residual, own=False)
        else:
            sweep(state, k0, residual)
        for j in range(KRYLOV):
            if final:
                send_movers(j + 1, krylov[j])
            sweep(krylov[j], krylov[j + 1], jacobian, ring=j < KRYLOV - 1)
        def products(r, sums):
            for c in range(1, cols + 1):
                values = [field[r, c] for field in krylov]
                new = []
                for (i, j), acc in zip(PAIRS, sums):
                    value = values[i] * values[j]
                    new.append(acc + (value[:, :half] + value[:, half:]))
                sums = tuple(new)
            return sums

        sums = lax.fori_loop(
            1, rows + 1, products, tuple(jnp.zeros((species, half), jnp.float32) for _ in PAIRS)
        )
        line = jnp.zeros((1, 128), jnp.float32)
        for at, acc in enumerate(sums):
            value = jnp.sum(jnp.sum(acc, axis=0, keepdims=True), axis=1, keepdims=True)
            line = line + jnp.where(out_lane == at, value, 0.0)

        gram_a[newton_step, band] = line

        def send_a(d, slot, target):
            return pltpu.make_async_remote_copy(
                src_ref=gram_a.at[newton_step, slot],
                dst_ref=gram_a.at[newton_step, slot],
                send_sem=a_send.at[newton_step, d],
                recv_sem=a_recv.at[newton_step, d],
                device_id={"grp": target},
                device_id_type=MESH,
            )

        def send_b(d, slot, target):
            return pltpu.make_async_remote_copy(
                src_ref=gram_b.at[newton_step, slot],
                dst_ref=gram_b.at[newton_step, slot],
                send_sem=b_send.at[newton_step, d],
                recv_sem=b_recv.at[newton_step, d],
                device_id={"patch": target},
                device_id_type=MESH,
            )

        for d in range(1, bands):
            send_a(d, band, lax.rem(band + d, bands)).start()
        for d in range(1, bands):
            send_a(d, lax.rem(band + bands - d, bands), band).wait_recv()
        part = gram_a[newton_step, 0]
        for d in range(1, bands):
            part = part + gram_a[newton_step, d]
        gram_b[newton_step, me] = part

        @pl.loop(1, owners)
        def _(d):
            send_b(d, me, lax.rem(me + d, owners)).start()

        @pl.loop(1, owners)
        def _(d):
            send_b(d, lax.rem(me + owners - d, owners), me).wait_recv()

        whole = gram_b[newton_step, 0]
        for d in range(1, owners):
            whole = whole + gram_b[newton_step, d]
        gram = {
            pair: jnp.sum(jnp.where(out_lane == at, whole, 0.0), axis=1, keepdims=True)
            for at, pair in enumerate(PAIRS)
        }
        weights = [
            jnp.broadcast_to(w, (1, surface)) for w in krylov_weights(gram)
        ]

        def update(r, c, lanes):
            return state[r, c, :, lanes] + (
                weights[0][:, : lanes.size] * k0[r, c, :, lanes]
                + weights[1][:, : lanes.size] * k1[r, c, :, lanes]
                + weights[2][:, : lanes.size] * k2[r, c, :, lanes]
            )

        if newton_step == 0:
            for at, (dx, dy) in enumerate(DIRECTIONS):
                @pl.when(exists(dx, dy))
                def _():
                    for f in range(2):
                        halo(f, at).wait_send()

        if not final:
            for c in range(ext_cols):
                state[0, c, :, high] = update(0, c, high)
                state[ext_rows - 1, c, :, low] = update(ext_rows - 1, c, low)

            @pl.loop(1, rows + 1)
            def _(r):
                for c in range(ext_cols):
                    state[r, c] = update(r, c, full)
        else:
            for r in range(1, rows + 1):
                for c in range(1, cols + 1):
                    stays = new_owner(r, c) == me
                    emit(
                        (r - 1) * cols + c - 1, jnp.where(stays, update(r, c, full), 0.0)
                    )

        for d in range(1, bands):
            send_a(d, band, band).wait_send()

        @pl.loop(1, owners)
        def _(d):
            send_b(d, me, me).wait_send()

    for side, step in enumerate((1, -1)):
        place = slots + side * MOVE_CAP

        @pl.when(exists(-step, 0))
        def _():
            for part in range(KRYLOV + 1):
                move(part, side, step).wait_recv()
            for m in range(MOVE_CAP):
                emit(place + m, landing[0, side, m] + (
                    weights[0] * landing[1, side, m]
                    + weights[1] * landing[2, side, m]
                    + weights[2] * landing[3, side, m]
                ))

        @pl.when(jnp.logical_not(exists(-step, 0)))
        def _():
            for m in range(MOVE_CAP):
                emit(place + m, jnp.zeros((species, surface), jnp.float32))

        @pl.when(exists(step, 0))
        def _():
            for part in range(KRYLOV + 1):
                move(part, side, step).wait_send()


def per_device(owners, bands, previous, predicted, new_owner, levels, diffusion, decay, reaction):
    patches, species, surface = previous.shape[2:]
    cols = patches // ROWS
    ext = (ROWS + 2, cols + 2, species, surface)
    linear = (patches * species * 2, surface // 2)
    slots = patches + 2 * MOVE_CAP
    vmem = pl.BlockSpec(memory_space=pltpu.VMEM)
    smem = pl.BlockSpec(memory_space=pltpu.SMEM)
    anywhere = pl.BlockSpec(memory_space=pl.ANY)
    dma = pltpu.SemaphoreType.DMA
    result = pl.pallas_call(
        functools.partial(kernel, owners, bands),
        out_shape=jax.ShapeDtypeStruct((species * slots * 2, surface // 2), jnp.float32),
        in_specs=[smem, smem, vmem, vmem, vmem, anywhere, anywhere],
        out_specs=vmem,
        scratch_shapes=[
            *[pltpu.VMEM(ext, jnp.float32) for _ in range(KRYLOV + 3)],
            pltpu.VMEM((ROWS + 2, cols + 2, 8, surface), jnp.float32),
            pltpu.VMEM((NEWTON, bands, 1, 128), jnp.float32),
            pltpu.VMEM((NEWTON, owners, 1, 128), jnp.float32),
            pltpu.VMEM((KRYLOV + 1, 2, MOVE_CAP, species, surface), jnp.float32),
            pltpu.VMEM((KRYLOV + 1, 2, MOVE_CAP, species, surface), jnp.float32),
            pltpu.VMEM((2, 2, ROWS // 2, species, surface), jnp.float32),
            pltpu.VMEM((2, 2, ROWS // 2, species, surface), jnp.float32),
            pltpu.VMEM((2, *linear), jnp.float32),
            dma((2,)),
            dma((2, len(DIRECTIONS))),
            dma((2, len(DIRECTIONS))),
            dma((NEWTON, bands)),
            dma((NEWTON, bands)),
            dma((NEWTON, owners)),
            dma((NEWTON, owners)),
            dma((KRYLOV + 1, 2)),
            dma((KRYLOV + 1, 2)),
        ],
        compiler_params=pltpu.CompilerParams(collective_id=0, has_side_effects=True),
    )(
        new_owner,
        levels,
        diffusion.reshape(1, species),
        decay.reshape(1, species),
        reaction,
        previous.reshape(linear),
        predicted.reshape(linear),
    )
    result = result.reshape(species, slots // 8, 2, 8, surface // 2)
    return result.transpose(1, 3, 0, 2, 4).reshape(1, 1, slots, species, surface)


def solution(mesh):
    placed = (P("grp", "patch"), P("grp", "patch"), P(), P(), P(), P(), P())
    return jax.shard_map(
        functools.partial(per_device, mesh.shape["patch"], mesh.shape["grp"]),
        mesh=mesh,
        in_specs=placed,
        out_specs=P("grp", "patch"),
        check_vma=False,
    )
```

```python
import functools

import jax
import jax.numpy as jnp
from jax import lax
from jax.experimental import pallas as pl
from jax.experimental.pallas import tpu as pltpu
from jax.sharding import PartitionSpec as P

CELLS = 16
ROWS = 4
MOVE_CAP = 2
KRYLOV = 3
NEWTON = 2

step_rate = 4.0
epsilon = 1e-12
SHIFT = 16.0
SCALE = 64.0
PAIRS = [(i, j) for j in range(KRYLOV + 1) for i in range(j + 1)]
DIRECTIONS = [(1, 0), (-1, 0), (1, 1), (-1, -1), (1, -1), (-1, 1), (0, 1), (0, -1)]


def small_solve(matrix, vector):
    dimension = len(vector)
    matrix = [list(line) for line in matrix]
    vector = list(vector)
    for column_at in range(dimension):
        for target in range(column_at + 1, dimension):
            factor = matrix[target][column_at] / matrix[column_at][column_at]
            for k in range(column_at, dimension):
                matrix[target][k] = matrix[target][k] - factor * matrix[column_at][k]
            vector[target] = vector[target] - factor * vector[column_at]
    answer = [None] * dimension
    for column_at in reversed(range(dimension)):
        running = vector[column_at]
        for later in range(column_at + 1, dimension):
            running = running - matrix[column_at][later] * answer[later]
        answer[column_at] = running / matrix[column_at][column_at]
    return answer


def add(a, b):
    return b if a is None else a if b is None else a + b


def total(terms):
    result = None
    for term in terms:
        result = add(result, term)
    return result


def krylov_weights(gram):
    size = KRYLOV + 1

    def inner(a, b):
        return total(
            a[i] * b[j] * gram[min(i, j), max(i, j)]
            for i in range(size)
            for j in range(size)
            if a[i] is not None and b[j] is not None
        )

    beta = jnp.sqrt(gram[0, 0] + epsilon)
    basis = [[-1.0 / beta] + [None] * KRYLOV]
    hess = [[None] * KRYLOV for _ in range(size)]
    for j in range(KRYLOV):
        current = basis[j]
        image = [None] * size
        for i in range(size):
            if current[i] is not None:
                image[i] = add(image[i], SHIFT * current[i])
                image[i + 1] = add(image[i + 1], SCALE * current[i])
        coeffs = [inner(image, vector) for vector in basis]
        for i, vector in enumerate(basis):
            hess[i][j] = coeffs[i]
            image = [
                a if b is None else a - coeffs[i] * b for a, b in zip(image, vector)
            ]
        height = jnp.sqrt(jnp.maximum(inner(image, image), 0.0) + epsilon)
        hess[j + 1][j] = height
        basis.append([None if a is None else a / height for a in image])
    normal = [
        [
            total(
                hess[k][a] * hess[k][b]
                for k in range(size)
                if hess[k][a] is not None and hess[k][b] is not None
            )
            for b in range(KRYLOV)
        ]
        for a in range(KRYLOV)
    ]
    y = small_solve(normal, [beta * hess[0][b] for b in range(KRYLOV)])
    return [
        total(y[j] * basis[j][i] for j in range(KRYLOV) if basis[j][i] is not None)
        for i in range(KRYLOV)
    ]


def kernel(
    owners, bands, owner_s, level_s, diff_in, decay_in, react_in, prev_in, pred_in, out,
    state, before, k0, k1, k2, k3, face, gram_a, gram_b, movers, landing, strip_out, strip_in, stage,
    local_sem, halo_send, halo_recv, a_send, a_recv, b_send, b_recv, move_send, move_recv,
):
    ext_rows, ext_cols, species, surface = state.shape
    rows, cols = ext_rows - 2, ext_cols - 2
    me = lax.axis_index("patch")
    band = lax.axis_index("grp")
    MESH = pl.DeviceIdType.MESH

    def exists(dx, dy):
        tests = []
        if dx:
            tests.append(me < owners - 1 if dx > 0 else me > 0)
        if dy:
            tests.append(band < bands - 1 if dy > 0 else band > 0)
        return functools.reduce(jnp.logical_and, tests)

    barrier = pltpu.get_barrier_semaphore()
    for d in range(1, bands):
        pl.semaphore_signal(
            barrier, inc=1, device_id={"grp": lax.rem(band + d, bands)}, device_id_type=MESH
        )

    @pl.loop(1, owners)
    def _(d):
        pl.semaphore_signal(
            barrier, inc=1, device_id={"patch": lax.rem(me + d, owners)}, device_id_type=MESH
        )

    for dx, dy in DIRECTIONS:
        if dx and dy:
            @pl.when(exists(dx, dy))
            def _():
                pl.semaphore_signal(
                    barrier, inc=1, device_id={"patch": me + dx, "grp": band + dy},
                    device_id_type=MESH,
                )

    fields = ((pred_in, state), (prev_in, before))
    own = [
        pltpu.make_async_copy(src, stage.at[f], local_sem.at[f])
        for f, (src, dst) in enumerate(fields)
    ]
    for copy in own:
        copy.start()

    half = surface // 2
    low, high = pl.ds(0, half), pl.ds(half, half)
    pairs = rows // 2

    def span(delta, length):
        if delta == 0:
            return pl.ds(1, length), pl.ds(1, length)
        if delta > 0:
            return pl.ds(length, 1), pl.ds(0, 1)
        return pl.ds(1, 1), pl.ds(length + 1, 1)

    def halo(f, at):
        dx, dy = DIRECTIONS[at]
        field = fields[f][1]
        if dy == 0:
            side = 0 if dx > 0 else 1
            source, target = strip_out.at[f, side], strip_in.at[f, side]
        else:
            lanes = high if dy > 0 else low
            col_from, col_to = span(dx, cols)
            row_from, row_to = span(dy, rows)
            source = field.at[row_from, col_from, :, lanes]
            target = field.at[row_to, col_to, :, lanes]
        return pltpu.make_async_remote_copy(
            src_ref=source,
            dst_ref=target,
            send_sem=halo_send.at[f, at],
            recv_sem=halo_recv.at[f, at],
            device_id={"patch": me + dx, "grp": band + dy},
            device_id_type=MESH,
        )

    lane = lax.broadcasted_iota(jnp.int32, (1, surface), 1)
    cell_col, cell_row = lane % CELLS, lane // CELLS
    right_half = cell_col >= CELLS // 2

    for f in range(2):
        own[f].wait()
        field = fields[f][1]
        for r in range(rows):
            for c in range(cols):
                for part, lanes in enumerate((low, high)):
                    first = (r * cols + c) * species * 2 + part
                    field[r + 1, c + 1, :, lanes] = stage[
                        f, pl.ds(first, species, stride=2), :
                    ]
        for k in range(pairs):
            first, second = field[2 * k + 1, cols], field[2 * k + 2, cols]
            strip_out[f, 0, k] = jnp.where(
                right_half, first, pltpu.roll(second, surface - CELLS // 2, 1)
            )
            first, second = field[2 * k + 1, 1], field[2 * k + 2, 1]
            strip_out[f, 1, k] = jnp.where(
                right_half, pltpu.roll(second, CELLS // 2, 1), first
            )

    def one(dx, dy):
        return jnp.where(exists(dx, dy), 1, 0)

    corners = (one(1, 0) + one(-1, 0)) * (one(0, 1) + one(0, -1))
    pl.semaphore_wait(barrier, bands - 1 + owners - 1 + corners)
    for at, (dx, dy) in enumerate(DIRECTIONS):
        @pl.when(exists(dx, dy))
        def _():
            halo(0, at).start()

        @pl.when(jnp.logical_not(exists(-dx, -dy)))
        def _():
            row_to, col_to = span(dy, rows)[1], span(dx, cols)[1]
            lanes = pl.ds(0, surface) if dy == 0 else high if dy > 0 else low
            shape = (row_to.size, col_to.size, species, lanes.size)
            for f in range(2):
                fields[f][1][row_to, col_to, :, lanes] = jnp.zeros(shape, jnp.float32)

    for at, (dx, dy) in enumerate(DIRECTIONS):
        @pl.when(exists(dx, dy))
        def _():
            halo(1, at).start()

    west_edge, east_edge = cell_col == 0, cell_col == CELLS - 1
    south_edge, north_edge = cell_row == 0, cell_row == CELLS - 1
    diagonal = lax.broadcasted_iota(jnp.int32, (species, species), 0) == (
        lax.broadcasted_iota(jnp.int32, (species, species), 1)
    )

    def column(ref):
        return jnp.sum(jnp.where(diagonal, ref[...], 0.0), axis=1, keepdims=True)

    diffusion, decay = column(diff_in), column(decay_in)
    kind = lax.broadcasted_iota(jnp.int32, (species, 1), 0)
    rate = jnp.where(kind < species - 1, step_rate, 0.0)
    reaction = react_in[...]
    reaction_a = reaction * (1.0 / SCALE)
    diffusion_a = diffusion * (1.0 / SCALE)
    decay_a = decay * (3.0 / SCALE)
    rate_a = (rate - SHIFT) * (1.0 / SCALE)

    def kappa(r, c):
        row = jnp.clip(band * rows + r - 1, 0, bands * rows - 1)
        col = jnp.clip(me * cols + c - 1, 0, owners * cols - 1)
        level = level_s[row // rows, col // cols, (row % rows) * cols + col % cols]
        return jnp.where(level == 0, 1.0, jnp.where(level == 1, 4.0, 16.0))

    @pl.loop(0, ext_rows)
    def _(r):
        for c in range(ext_cols):
            mid = kappa(r, c)
            west = jnp.where(west_edge, 0.5 * (mid + kappa(r, c - 1)), mid)
            east = jnp.where(east_edge, 0.5 * (mid + kappa(r, c + 1)), mid)
            south = jnp.where(south_edge, 0.5 * (mid + kappa(r - 1, c)), mid)
            north = jnp.where(north_edge, 0.5 * (mid + kappa(r + 1, c)), mid)
            for d, value in enumerate((west, east, south, north)):
                face[r, c, pl.ds(d, 1), :] = value
            face[r, c, pl.ds(4, 1), :] = west + east + south + north

    def receive(f):
        for at, (dx, dy) in enumerate(DIRECTIONS):
            @pl.when(exists(-dx, -dy))
            def _():
                halo(f, at).wait_recv()
                if dy == 0:
                    for k in range(pairs):
                        strip = strip_in[f, 0 if dx > 0 else 1, k]
                        at_col = 0 if dx > 0 else cols + 1
                        shift = CELLS // 2 if dx > 0 else surface - CELLS // 2
                        fields[f][1][2 * k + 1, at_col] = strip
                        fields[f][1][2 * k + 2, at_col] = pltpu.roll(strip, shift, 1)

    def inside(r, c):
        row, col = band * rows + r - 1, me * cols + c - 1
        good = (row >= 0) & (row < bands * rows) & (col >= 0) & (col < owners * cols)
        return jnp.where(good, 1.0, 0.0)

    def edges(width):
        column = lax.broadcasted_iota(jnp.int32, (1, width), 1)
        return (
            column % CELLS == 0,
            column % CELLS == CELLS - 1,
            column < CELLS,
            column >= width - CELLS,
        )

    whole_edges, half_edges = edges(surface), edges(half)

    def patch(src, dst, finish, r, c, lanes, below, above):
        width = lanes.size
        at_west, at_east, at_south, at_north = (
            whole_edges if width == surface else half_edges
        )
        x = src[r, c, :, lanes]
        left = src[r, max(c - 1, 0), :, lanes]
        right = src[r, min(c + 1, ext_cols - 1), :, lanes]
        under = x if below is None else src[below[0], c, :, below[1]]
        over = x if above is None else src[above[0], c, :, above[1]]
        west = jnp.where(
            at_west, pltpu.roll(left, width - CELLS + 1, 1), pltpu.roll(x, 1, 1)
        )
        east = jnp.where(
            at_east, pltpu.roll(right, CELLS - 1, 1), pltpu.roll(x, width - 1, 1)
        )
        south = pltpu.roll(jnp.where(at_north, under, x), CELLS, 1)
        north = pltpu.roll(jnp.where(at_south, over, x), width - CELLS, 1)
        lap = (
            face[r, c, pl.ds(0, 1), lanes] * west
            + face[r, c, pl.ds(1, 1), lanes] * east
            + face[r, c, pl.ds(2, 1), lanes] * south
            + face[r, c, pl.ds(3, 1), lanes] * north
            - face[r, c, pl.ds(4, 1), lanes] * x
        )
        dst[r, c, :, lanes] = finish(r, c, lanes, x, lap)

    full = pl.ds(0, surface)

    def sweep(src, dst, finish, own=True, ring=True):
        columns = list(range(1, cols + 1)) if own else []
        if ring:
            columns = [0, *columns, cols + 1]

        def masked(r, c, lanes, x, lap):
            return finish(r, c, lanes, x, lap) * inside(r, c)

        last = ext_rows - 1
        if ring:
            for c in range(ext_cols):
                patch(src, dst, masked, 0, c, high, None, (1, low))
                patch(src, dst, masked, last, c, low, (last - 1, high), None)

        @pl.loop(1, rows + 1, unroll=True)
        def _(r):
            for c in columns:
                patch(
                    src, dst, masked if c in (0, cols + 1) else finish,
                    r, c, full, (r - 1, full), (r + 1, full),
                )

    def split(value):
        big = value.astype(jnp.bfloat16)
        return big, (value - big.astype(jnp.float32)).astype(jnp.bfloat16)

    react_parts, react_a_parts = split(reaction), split(reaction_a)

    def mixing(parts, x):
        react_big, react_small = parts
        big, small = split(x)

        def product(a, b):
            return jnp.dot(a, b, preferred_element_type=jnp.float32)

        return product(react_small, big) + product(react_big, small) + product(react_big, big)

    def residual(r, c, lanes, x, lap):
        old = before[r, c, :, lanes]
        return rate * (x - old) - diffusion * lap - mixing(react_parts, x) + decay * (x * x * x)

    def jacobian(r, c, lanes, x, lap):
        u = state[r, c, :, lanes]
        return (rate_a + decay_a * (u * u)) * x - diffusion_a * lap - mixing(react_a_parts, x)

    krylov = (k0, k1, k2, k3)
    out_lane = lax.broadcasted_iota(jnp.int32, (1, 128), 1)

    def new_owner(r, c):
        return owner_s[band, me, (r - 1) * cols + c - 1]

    slots = rows * cols

    def emit(slot, value):
        for part in range(2):
            first = slot // 8 * 16 + part * 8 + slot % 8
            out[pl.ds(first, species, stride=2 * (slots + 2 * MOVE_CAP)), :] = (
                value[:, part * half : (part + 1) * half]
            )

    def move(part, side, step):
        return pltpu.make_async_remote_copy(
            src_ref=movers.at[part, side],
            dst_ref=landing.at[part, side],
            send_sem=move_send.at[part, side],
            recv_sem=move_recv.at[part, side],
            device_id={"patch": me + step},
            device_id_type=MESH,
        )

    def send_movers(part, field):
        for side, (c, step) in enumerate(((cols, 1), (1, -1))):
            rank = jnp.int32(0)
            packed = [jnp.zeros((species, surface), jnp.float32) for _ in range(MOVE_CAP)]
            for r in range(1, rows + 1):
                moving = new_owner(r, c) == me + step
                for m in range(MOVE_CAP):
                    packed[m] = jnp.where(moving & (rank == m), field[r, c], packed[m])
                rank = rank + jnp.where(moving, 1, 0)
            for m in range(MOVE_CAP):
                movers[part, side, m] = packed[m]
        for side, step in enumerate((1, -1)):
            @pl.when(exists(step, 0))
            def _():
                move(part, side, step).start()

    for newton_step in range(NEWTON):
        final = newton_step == NEWTON - 1
        if final:
            send_movers(0, state)
        if newton_step == 0:
            receive(0)
            sweep(state, k0, residual, ring=False)
            receive(1)
            sweep(state, k0, residual, own=False)
        else:
            sweep(state, k0, residual)
        for j in range(KRYLOV):
            if final:
                send_movers(j + 1, krylov[j])
            sweep(krylov[j], krylov[j + 1], jacobian, ring=j < KRYLOV - 1)
        def products(r, sums):
            for c in range(1, cols + 1):
                values = [field[r, c] for field in krylov]
                new = []
                for (i, j), acc in zip(PAIRS, sums):
                    value = values[i] * values[j]
                    new.append(acc + (value[:, :half] + value[:, half:]))
                sums = tuple(new)
            return sums

        sums = lax.fori_loop(
            1, rows + 1, products, tuple(jnp.zeros((species, half), jnp.float32) for _ in PAIRS)
        )
        line = jnp.zeros((1, 128), jnp.float32)
        for at, acc in enumerate(sums):
            value = jnp.sum(jnp.sum(acc, axis=0, keepdims=True), axis=1, keepdims=True)
            line = line + jnp.where(out_lane == at, value, 0.0)

        gram_a[newton_step, band] = line

        def send_a(d, slot, target):
            return pltpu.make_async_remote_copy(
                src_ref=gram_a.at[newton_step, slot],
                dst_ref=gram_a.at[newton_step, slot],
                send_sem=a_send.at[newton_step, d],
                recv_sem=a_recv.at[newton_step, d],
                device_id={"grp": target},
                device_id_type=MESH,
            )

        def send_b(d, slot, target):
            return pltpu.make_async_remote_copy(
                src_ref=gram_b.at[newton_step, slot],
                dst_ref=gram_b.at[newton_step, slot],
                send_sem=b_send.at[newton_step, d],
                recv_sem=b_recv.at[newton_step, d],
                device_id={"patch": target},
                device_id_type=MESH,
            )

        for d in range(1, bands):
            send_a(d, band, lax.rem(band + d, bands)).start()
        for d in range(1, bands):
            send_a(d, lax.rem(band + bands - d, bands), band).wait_recv()
        part = gram_a[newton_step, 0]
        for d in range(1, bands):
            part = part + gram_a[newton_step, d]
        gram_b[newton_step, me] = part

        @pl.loop(1, owners)
        def _(d):
            send_b(d, me, lax.rem(me + d, owners)).start()

        @pl.loop(1, owners)
        def _(d):
            send_b(d, lax.rem(me + owners - d, owners), me).wait_recv()

        whole = gram_b[newton_step, 0]
        for d in range(1, owners):
            whole = whole + gram_b[newton_step, d]
        gram = {
            pair: jnp.sum(jnp.where(out_lane == at, whole, 0.0), axis=1, keepdims=True)
            for at, pair in enumerate(PAIRS)
        }
        weights = [
            jnp.broadcast_to(w, (1, surface)) for w in krylov_weights(gram)
        ]

        def update(r, c, lanes):
            return state[r, c, :, lanes] + (
                weights[0][:, : lanes.size] * k0[r, c, :, lanes]
                + weights[1][:, : lanes.size] * k1[r, c, :, lanes]
                + weights[2][:, : lanes.size] * k2[r, c, :, lanes]
            )

        if newton_step == 0:
            for at, (dx, dy) in enumerate(DIRECTIONS):
                @pl.when(exists(dx, dy))
                def _():
                    for f in range(2):
                        halo(f, at).wait_send()

        if not final:
            for c in range(ext_cols):
                state[0, c, :, high] = update(0, c, high)
                state[ext_rows - 1, c, :, low] = update(ext_rows - 1, c, low)

            @pl.loop(1, rows + 1)
            def _(r):
                for c in range(ext_cols):
                    state[r, c] = update(r, c, full)
        else:
            for r in range(1, rows + 1):
                for c in range(1, cols + 1):
                    stays = new_owner(r, c) == me
                    emit(
                        (r - 1) * cols + c - 1, jnp.where(stays, update(r, c, full), 0.0)
                    )

        for d in range(1, bands):
            send_a(d, band, band).wait_send()

        @pl.loop(1, owners)
        def _(d):
            send_b(d, me, me).wait_send()

    for side, step in enumerate((1, -1)):
        place = slots + side * MOVE_CAP

        @pl.when(exists(-step, 0))
        def _():
            for part in range(KRYLOV + 1):
                move(part, side, step).wait_recv()
            for m in range(MOVE_CAP):
                emit(place + m, landing[0, side, m] + (
                    weights[0] * landing[1, side, m]
                    + weights[1] * landing[2, side, m]
                    + weights[2] * landing[3, side, m]
                ))

        @pl.when(jnp.logical_not(exists(-step, 0)))
        def _():
            for m in range(MOVE_CAP):
                emit(place + m, jnp.zeros((species, surface), jnp.float32))

        @pl.when(exists(step, 0))
        def _():
            for part in range(KRYLOV + 1):
                move(part, side, step).wait_send()


def per_device(owners, bands, previous, predicted, new_owner, levels, diffusion, decay, reaction):
    patches, species, surface = previous.shape[2:]
    cols = patches // ROWS
    ext = (ROWS + 2, cols + 2, species, surface)
    linear = (patches * species * 2, surface // 2)
    slots = patches + 2 * MOVE_CAP
    vmem = pl.BlockSpec(memory_space=pltpu.VMEM)
    smem = pl.BlockSpec(memory_space=pltpu.SMEM)
    anywhere = pl.BlockSpec(memory_space=pl.ANY)
    dma = pltpu.SemaphoreType.DMA
    result = pl.pallas_call(
        functools.partial(kernel, owners, bands),
        out_shape=jax.ShapeDtypeStruct((species * slots * 2, surface // 2), jnp.float32),
        in_specs=[smem, smem, vmem, vmem, vmem, anywhere, anywhere],
        out_specs=vmem,
        scratch_shapes=[
            *[pltpu.VMEM(ext, jnp.float32) for _ in range(KRYLOV + 3)],
            pltpu.VMEM((ROWS + 2, cols + 2, 8, surface), jnp.float32),
            pltpu.VMEM((NEWTON, bands, 1, 128), jnp.float32),
            pltpu.VMEM((NEWTON, owners, 1, 128), jnp.float32),
            pltpu.VMEM((KRYLOV + 1, 2, MOVE_CAP, species, surface), jnp.float32),
            pltpu.VMEM((KRYLOV + 1, 2, MOVE_CAP, species, surface), jnp.float32),
            pltpu.VMEM((2, 2, ROWS // 2, species, surface), jnp.float32),
            pltpu.VMEM((2, 2, ROWS // 2, species, surface), jnp.float32),
            pltpu.VMEM((2, *linear), jnp.float32),
            dma((2,)),
            dma((2, len(DIRECTIONS))),
            dma((2, len(DIRECTIONS))),
            dma((NEWTON, bands)),
            dma((NEWTON, bands)),
            dma((NEWTON, owners)),
            dma((NEWTON, owners)),
            dma((KRYLOV + 1, 2)),
            dma((KRYLOV + 1, 2)),
        ],
        compiler_params=pltpu.CompilerParams(collective_id=0, has_side_effects=True),
    )(
        new_owner,
        levels,
        diffusion.reshape(1, species),
        decay.reshape(1, species),
        reaction,
        previous.reshape(linear),
        predicted.reshape(linear),
    )
    result = result.reshape(species, slots // 8, 2, 8, surface // 2)
    return result.transpose(1, 3, 0, 2, 4).reshape(1, 1, slots, species, surface)


def solution(mesh):
    placed = (P("grp", "patch"), P("grp", "patch"), P(), P(), P(), P(), P())
    return jax.shard_map(
        functools.partial(per_device, mesh.shape["patch"], mesh.shape["grp"]),
        mesh=mesh,
        in_specs=placed,
        out_specs=P("grp", "patch"),
        check_vma=False,
    )
```
